512 devices in a mesh: req: 128 (over z, y, core), tp: 4 (over x).
Axes of the slice: x: 4, y: 8, z: 8, core: 2. Of those that a mesh axis runs over, the one named last changes fastest.
Arguments:
- prompt_query: bfloat16 [32768, 2048], P('req', 'tp')
- prompt_key_value: bfloat16 [32768, 4, 256], P('req', 'tp')
- prompt_segment_index: int32 [128, 256], P('req'), may hold values from 0 to 3, never falling along the last dimension, each value on 1 to 128 neighbouring positions
- decoder_query: bfloat16 [256, 2048], P('req', 'tp')
- decoder_key_value: bfloat16 [256, 4, 256], P('req', 'tp')
- key_value_cache: bfloat16 [256, 512, 4, 256], P('req', None, 'tp')
- live_cache_length: int32 [256], P('req'), may hold values from 128 to 512, as said below
- rebuild_hidden_state: bfloat16 [16384, 2048], P('req'), may hold values from -6 to 6
- owner_dest: int32 [128, 128], P('req'), may hold values from -1 to 127, as said below
- miss_pos: int32 [128, 128], P('req'), may hold values from -1 to 1023, as said below
- key_value_weight: bfloat16 [2048, 4, 256], P(None, 'tp'), may hold values from -0.125 to 0.125
- out_weight: bfloat16 [2048, 2048], P('tp'), may hold values from -0.125 to 0.125
Outputs:
- prompt_out: bfloat16 [32768, 2048], P('req', 'tp')
- dec_out: bfloat16 [256, 2048], P('req', 'tp')
The draws below stay inside these ranges and needn't reach their ends.
Inputs may be any that keep to these rules, and one draw needn't show every extreme that they name: `prompt_segment_index`: each device's numbers never fall along the row; each prompt has 1 to 128 tokens and one has exactly that many. Positions 0 to live_cache_length - 1 of a decoder are live; some decoder has exactly 512. Row r of device o's list goes to device owner_dest[o, r], or nowhere if -1. The rows of one device going to one device are exactly rows g * 2 to g * 2 + 1 of one block g, all sent or all -1; some device receives 2 rows from each of 64 devices. A row r that device o sends to device e fills cache slot miss_pos[e, r] = decoder * 512 + position of device e; miss_pos[e, r] is -1 exactly where no device sends row r to e. The live slots of one device are distinct and below that decoder's live_cache_length.
All inputs are finite; a program needn't handle non-finite values.
Results may differ from the reference program's by a relative error of at most 0.019.
Values may be sent and summed in bfloat16 or wider, within the bound.
No kernel may reach another device: no remote copies, remote signals or barrier semaphores. Data moves between devices by JAX's collectives and lax.ppermute only.
A program may use at most 64 MiB of HBM per device.

```python
import math
import jax
import jax.numpy as jnp
import numpy as np
from jax import lax

MODEL_WIDTH = 2048
QUERY_HEADS = 16
KEY_VALUE_HEADS = 4
HEAD_WIDTH = 128
PROMPT_TOKENS = 256
PROMPTS = 4
DECODERS_PER_REQ = 2
CACHE_SLOTS = 512
CAP = 2
RSLOTS = 128
N_REQ = 128


def recompute_plan(key):
    base_key = jax.random.fold_in(key, 101)
    age_key, longest_key, offset_key, group_key, busiest_key, score_key = jax.random.split(base_key, 6)
    groups_half = N_REQ // 2
    slot_count = DECODERS_PER_REQ * CACHE_SLOTS
    decoders_all = N_REQ * DECODERS_PER_REQ
    ages = jax.random.randint(age_key, (decoders_all,), CACHE_SLOTS // 4, CACHE_SLOTS + 1)
    longest_dev = jax.random.randint(longest_key, (), 0, N_REQ)
    longest = longest_dev * DECODERS_PER_REQ + DECODERS_PER_REQ - 1
    ages = jnp.where(jnp.arange(decoders_all) == longest, CACHE_SLOTS, ages).astype(jnp.int32)
    offsets = jax.random.permutation(offset_key, N_REQ)[:groups_half]
    live_groups = jax.random.randint(group_key, (N_REQ,), max(3 * groups_half // 4, 1), groups_half + 1)
    busiest = jax.random.randint(busiest_key, (), 0, N_REQ)
    live_groups = jnp.where(jnp.arange(N_REQ) == busiest, groups_half, live_groups)
    age_dev = ages.reshape(N_REQ, DECODERS_PER_REQ)
    slot_ids = jnp.arange(slot_count, dtype=jnp.int32)
    alive_mask = (slot_ids % CACHE_SLOTS)[None, :] < age_dev[:, slot_ids // CACHE_SLOTS]
    scores = jax.random.randint(score_key, (N_REQ, slot_count), 0, 2 ** 19) * slot_count + slot_ids[None, :]
    scores = jnp.where(alive_mask, scores, -1 - slot_ids[None, :])
    forced = (jnp.arange(N_REQ)[:, None] == longest_dev) & (slot_ids[None, :] == slot_count - 1)
    scores = jnp.where(forced, 2 ** 20 * slot_count, scores).astype(jnp.int32)
    chosen = lax.top_k(scores, CAP * groups_half)[1].astype(jnp.int32)
    list_index = jnp.arange(CAP * groups_half, dtype=jnp.int32)
    block_index = list_index // CAP
    missing = jnp.where(block_index[None, :] < live_groups[:, None], chosen, -1)
    owner_ids = jnp.arange(N_REQ, dtype=jnp.int32)[:, None]
    destination = (owner_ids - offsets[block_index][None, :]) % N_REQ
    destination = jnp.where(block_index[None, :] < live_groups[destination], destination, -1)
    return (ages, missing.astype(jnp.int32), destination.astype(jnp.int32))


def draw_live_cache_length(key, part):
    return recompute_plan(key)[0]


def draw_miss_pos(key, part):
    return recompute_plan(key)[1]


def draw_owner_dest(key, part):
    return recompute_plan(key)[2]


def prompt_key_rows(key):
    pair_key = jax.random.fold_in(key, 202)
    count_of_rows = N_REQ * PROMPT_TOKENS
    complete_shape = (count_of_rows, KEY_VALUE_HEADS, 2 * HEAD_WIDTH)
    pairs = jax.random.normal(pair_key, complete_shape, jnp.float32)
    return pairs


def draw_prompt_key_value(key, part):
    return prompt_key_rows(key).astype(jnp.bfloat16)


def draw_prompt_query(key, part):
    query_key = jax.random.fold_in(key, 212)
    count_of_rows = N_REQ * PROMPT_TOKENS
    complete_shape = (count_of_rows, QUERY_HEADS, HEAD_WIDTH)
    query_rows = 2.0 * jax.random.normal(query_key, complete_shape, jnp.float32)
    return query_rows.reshape(count_of_rows, QUERY_HEADS * HEAD_WIDTH).astype(jnp.bfloat16)


def decoder_key_rows(key):
    pair_key = jax.random.fold_in(key, 303)
    complete_shape = (N_REQ * DECODERS_PER_REQ, KEY_VALUE_HEADS, 2 * HEAD_WIDTH)
    pairs = jax.random.normal(pair_key, complete_shape, jnp.float32)
    return pairs


def draw_decoder_key_value(key, part):
    return decoder_key_rows(key).astype(jnp.bfloat16)


def draw_decoder_query(key, part):
    query_key = jax.random.fold_in(key, 404)
    count_of_rows = N_REQ * DECODERS_PER_REQ
    complete_shape = (count_of_rows, QUERY_HEADS, HEAD_WIDTH)
    query_rows = 2.0 * jax.random.normal(query_key, complete_shape, jnp.float32)
    return query_rows.reshape(count_of_rows, QUERY_HEADS * HEAD_WIDTH).astype(jnp.bfloat16)


def draw_key_value_cache(key, part):
    cache_key = jax.random.fold_in(key, 505)
    complete_shape = (N_REQ * DECODERS_PER_REQ, CACHE_SLOTS, KEY_VALUE_HEADS, 2 * HEAD_WIDTH)
    entries = jax.random.normal(cache_key, complete_shape, jnp.float32)
    return entries.astype(jnp.bfloat16)


def level_of(stream_key, dims, cuts, least, largest):
    def one(axis_at, blocks):
        steps = jax.random.uniform(jax.random.fold_in(jax.random.fold_in(stream_key, 6), axis_at), (blocks,), jnp.float32, least / len(cuts), largest / len(cuts))
        return jnp.repeat(jnp.exp(steps), dims[axis_at] // blocks).reshape((-1,) + (1,) * (len(dims) - axis_at - 1))

    gain = one(*cuts[0])
    for cut in cuts[1:]:
        gain = gain * one(*cut)
    return gain


def length_profile(count, total, most, lean):
    portions = [(1 << 20) // math.isqrt(standing ** lean) + 1 for standing in range(2, count + 1)]
    surplus, holding = total - most - (count - 1), [1] * (count - 1)
    while surplus > 0:
        movable = [i for i in range(count - 1) if holding[i] < most]
        whole, budget = sum([portions[i] for i in movable]), surplus
        for i in movable:
            more = min(most - holding[i], max(1, budget * portions[i] // whole), surplus)
            holding[i] = holding[i] + more
            surplus = surplus - more
    return np.array([most] + holding)


def uneven_parts(rng, amount, total, reach, lean):
    if amount == 2:
        one = jax.random.randint(rng, (), max(1, total - reach), min(reach, total - 1) + 1)
        return jnp.stack([one, total - one])
    tallies = jnp.asarray(length_profile(amount, total, reach, lean), jnp.int32)
    twos = (amount - 1) // 2
    source_of, taker = tallies[1:1 + 2 * twos:2], tallies[2:2 + 2 * twos:2]
    room = jnp.minimum(source_of - 1, reach - taker)
    passed = jax.random.randint(jax.random.fold_in(rng, 1), (twos,), 0, 1 << 20) % (room + 1)
    tallies = tallies.at[1:1 + 2 * twos:2].set(source_of - passed).at[2:2 + 2 * twos:2].set(taker + passed)
    return tallies[jax.random.permutation(jax.random.fold_in(rng, 2), amount)]


def centred(rng, dims, width, bound, cuts=(), held_as=jnp.bfloat16):
    values = jax.random.normal(rng, dims, jnp.float32) * width
    if len(cuts) > 0:
        values = level_of(rng, dims, cuts, -0.22, 0.18) * values
    return jnp.clip(values, min=-bound, max=bound).astype(held_as)


def setup_inputs(seed: int = 0) -> dict:
    seeds = jax.random.split(jax.random.key(seed), 13)
    return {
        "prompt_query": draw_prompt_query(jax.random.fold_in(seeds[12], 71), 0),
        "prompt_key_value": draw_prompt_key_value(jax.random.fold_in(seeds[12], 71), 0),
        "prompt_segment_index": jax.vmap(lambda own: jnp.searchsorted(jnp.cumsum(uneven_parts(own, PROMPTS, PROMPT_TOKENS, PROMPT_TOKENS // 2, 1)), jnp.arange(PROMPT_TOKENS), side="right"))(jax.random.split(seeds[2], N_REQ)).reshape((N_REQ, PROMPT_TOKENS)).astype(jnp.int32),
        "decoder_query": draw_decoder_query(jax.random.fold_in(seeds[12], 71), 0),
        "decoder_key_value": draw_decoder_key_value(jax.random.fold_in(seeds[12], 71), 0),
        "key_value_cache": draw_key_value_cache(jax.random.fold_in(seeds[12], 71), 0),
        "live_cache_length": draw_live_cache_length(jax.random.fold_in(seeds[12], 71), 0),
        "rebuild_hidden_state": centred(seeds[7], (N_REQ * RSLOTS, MODEL_WIDTH), 1.0, 6.0, ((0, 128),)),
        "owner_dest": draw_owner_dest(jax.random.fold_in(seeds[12], 71), 0),
        "miss_pos": draw_miss_pos(jax.random.fold_in(seeds[12], 71), 0),
        "key_value_weight": centred(seeds[10], (MODEL_WIDTH, KEY_VALUE_HEADS, 2 * HEAD_WIDTH), MODEL_WIDTH ** -0.5, 0.125, ((1, 4),)),
        "out_weight": centred(seeds[11], (QUERY_HEADS * HEAD_WIDTH, MODEL_WIDTH), (QUERY_HEADS * HEAD_WIDTH) ** -0.5, 0.125, ((0, 4),)),
    }


ROPE_BASE = 600000.0


def rotate(key_rows, position):
    half_width = key_rows.shape[-1] // 2
    frequency = ROPE_BASE ** (-2.0 * jnp.arange(half_width, dtype=jnp.float32) / key_rows.shape[-1])
    angles = position.astype(jnp.float32)[:, None, None] * frequency[None, None, :]
    front_half = key_rows[..., :half_width]
    back_half = key_rows[..., half_width:]
    cosine = jnp.cos(angles)
    sine_part = jnp.sin(angles)
    return jnp.concatenate([front_half * cosine - back_half * sine_part, back_half * cosine + front_half * sine_part], axis=-1)


def normalize(score_parts, self_score):
    row_peak = self_score
    for scores in score_parts:
        row_peak = jnp.maximum(row_peak, jnp.max(scores, axis=-1))
    own_exp = jnp.exp(self_score - row_peak)
    row_total = own_exp
    exponents = []
    for scores in score_parts:
        exponent = jnp.exp(scores - row_peak[..., None])
        exponents.append(exponent)
        row_total = row_total + jnp.sum(exponent, axis=-1)
    return (own_exp / row_total).astype(jnp.bfloat16), [(exponent / row_total[..., None]).astype(jnp.bfloat16) for exponent in exponents]


def reference(prompt_query, prompt_key_value, prompt_segment_index, decoder_query, decoder_key_value, key_value_cache, live_cache_length, rebuild_hidden_state, owner_dest, miss_pos, key_value_weight, out_weight):
    logit_scale = HEAD_WIDTH ** -0.5
    queries_per_group = QUERY_HEADS // KEY_VALUE_HEADS
    rebuilt_rows = jnp.dot(rebuild_hidden_state, key_value_weight.reshape(MODEL_WIDTH, KEY_VALUE_HEADS * 2 * HEAD_WIDTH), preferred_element_type=jnp.float32)
    rebuilt_rows = rebuilt_rows.astype(jnp.bfloat16).reshape(-1, KEY_VALUE_HEADS, 2 * HEAD_WIDTH)
    target_dev = owner_dest.reshape(-1)
    row_order = jnp.tile(jnp.arange(RSLOTS, dtype=jnp.int32), N_REQ)
    safe_dev = jnp.maximum(target_dev, 0)
    cache_slot = miss_pos[safe_dev, row_order]
    rotated = rotate(rebuilt_rows[..., :HEAD_WIDTH].astype(jnp.float32), cache_slot % CACHE_SLOTS).astype(jnp.bfloat16)
    rebuilt_rows = jnp.concatenate([rotated, rebuilt_rows[..., HEAD_WIDTH:]], axis=-1)
    total_slots = N_REQ * DECODERS_PER_REQ * CACHE_SLOTS
    target_position = jnp.where(target_dev >= 0, safe_dev * (DECODERS_PER_REQ * CACHE_SLOTS) + cache_slot, total_slots).astype(jnp.int32)
    updated_cache = key_value_cache.reshape(total_slots, KEY_VALUE_HEADS, 2 * HEAD_WIDTH).at[target_position].set(rebuilt_rows, mode="drop")
    updated_cache = updated_cache.reshape(N_REQ, DECODERS_PER_REQ, CACHE_SLOTS, KEY_VALUE_HEADS, 2 * HEAD_WIDTH)

    def decoder_step(inputs):
        query_rows, self_pair, cache_block, age_rows = inputs
        query_rows = query_rows.reshape(DECODERS_PER_REQ, KEY_VALUE_HEADS, queries_per_group, HEAD_WIDTH).astype(jnp.float32)
        self_pair = self_pair.astype(jnp.float32)
        cache_block = cache_block.astype(jnp.float32)
        self_score = jnp.einsum("siwr,sir->siw", query_rows, self_pair[..., :HEAD_WIDTH]) * logit_scale
        cache_score = jnp.einsum("bkgd,bckd->bkgc", query_rows, cache_block[..., :HEAD_WIDTH]) * logit_scale
        alive_mask = jnp.arange(CACHE_SLOTS)[None, :] < age_rows[:, None]
        cache_score = jnp.where(alive_mask[:, None, None, :], cache_score, -jnp.inf)
        own_weight, weight_list = normalize([cache_score], self_score)
        mixture = jnp.einsum("bkgc,bckd->bkgd", weight_list[0].astype(jnp.float32), cache_block[..., HEAD_WIDTH:])
        mixture = mixture + own_weight.astype(jnp.float32)[..., None] * self_pair[:, :, None, HEAD_WIDTH:]
        return mixture.astype(jnp.bfloat16).reshape(DECODERS_PER_REQ, QUERY_HEADS * HEAD_WIDTH)

    decoder_attention = lax.map(decoder_step, (decoder_query.reshape(N_REQ, DECODERS_PER_REQ, QUERY_HEADS * HEAD_WIDTH), decoder_key_value.reshape(N_REQ, DECODERS_PER_REQ, KEY_VALUE_HEADS, 2 * HEAD_WIDTH), updated_cache, live_cache_length.reshape(N_REQ, DECODERS_PER_REQ)))
    decoder_attention = decoder_attention.reshape(N_REQ * DECODERS_PER_REQ, QUERY_HEADS * HEAD_WIDTH)

    def prompt_step(inputs):
        query_rows, key_value, segment = inputs
        query_rows = query_rows.reshape(PROMPT_TOKENS, KEY_VALUE_HEADS, queries_per_group, HEAD_WIDTH).astype(jnp.float32)
        key_value = key_value.astype(jnp.float32)
        scores = jnp.einsum("ikgd,jkd->kgij", query_rows, key_value[..., :HEAD_WIDTH]) * logit_scale
        positions = jnp.arange(PROMPT_TOKENS)
        allowed = (segment[:, None] == segment[None, :]) & (positions[None, :] <= positions[:, None])
        scores = jnp.where(allowed, scores, -jnp.inf)
        row_peak = jnp.max(scores, axis=-1, keepdims=True)
        exponent = jnp.exp(scores - row_peak)
        weight = (exponent / jnp.sum(exponent, axis=-1, keepdims=True)).astype(jnp.bfloat16)
        mixture = jnp.einsum("kgij,jkd->ikgd", weight.astype(jnp.float32), key_value[..., HEAD_WIDTH:])
        return mixture.astype(jnp.bfloat16).reshape(PROMPT_TOKENS, QUERY_HEADS * HEAD_WIDTH)

    prompt_attention = lax.map(prompt_step, (prompt_query.reshape(N_REQ, PROMPT_TOKENS, QUERY_HEADS * HEAD_WIDTH), prompt_key_value.reshape(N_REQ, PROMPT_TOKENS, KEY_VALUE_HEADS, 2 * HEAD_WIDTH), prompt_segment_index))
    prompt_attention = prompt_attention.reshape(N_REQ * PROMPT_TOKENS, QUERY_HEADS * HEAD_WIDTH)
    prompt_out = jnp.dot(prompt_attention, out_weight, preferred_element_type=jnp.float32).astype(jnp.bfloat16)
    dec_out = jnp.dot(decoder_attention, out_weight, preferred_element_type=jnp.float32).astype(jnp.bfloat16)
    return (prompt_out, dec_out)
```

```python
import jax
import jax.numpy as jnp
import numpy as np
from jax import lax
from jax.experimental import pallas as pl
from jax.experimental.pallas import tpu as pltpu
from jax.sharding import PartitionSpec as P

CAP = 2
ROPE_BASE = 600000.0
F32 = jnp.float32
BF16 = jnp.bfloat16


def dot(a, b, ca, cb):
    return lax.dot_general(a, b, (((ca,), (cb,)), ((), ())), preferred_element_type=F32)


def call(kernel, outs, *args, scalars=()):
    vmem = pl.BlockSpec(memory_space=pltpu.VMEM)
    smem = pl.BlockSpec(memory_space=pltpu.SMEM)
    return pl.pallas_call(
        kernel,
        out_shape=outs,
        in_specs=[smem] * len(scalars) + [vmem] * len(args),
        out_specs=jax.tree.map(lambda _: vmem, outs),
    )(*scalars, *args)


def pack_kernel(hidden, weight, dest, out):
    peers, cap, width = out.shape
    rows = hidden.shape[0]
    rebuilt = dot(hidden[...], weight[...], 1, 0).astype(BF16)
    number = lax.broadcasted_iota(jnp.int32, (1, rows), 1)
    code = dest[...] * cap + number % cap
    code = jnp.where(dest[...] >= 0, code, -1)
    place = lax.broadcasted_iota(jnp.int32, (peers * cap, rows), 0)
    chosen = jnp.where(place == code, 1.0, 0.0).astype(BF16)
    packed = dot(chosen, rebuilt, 1, 0).astype(BF16)
    both = jnp.concatenate([packed, chosen], axis=1)
    out[...] = both.reshape(peers, cap, width)


def prompt_kernel(query, key_value, segment, weight, out):
    tokens, _ = query.shape
    head = key_value.shape[1] // 2
    groups = query.shape[1] // head
    parts, _, share = out.shape
    scale = head**-0.5
    same = jnp.where(
        lax.broadcasted_iota(jnp.int32, (8, tokens), 0) == segment[...], 1.0, 0.0
    ).astype(BF16)
    same = dot(same, same, 0, 0)
    row = lax.broadcasted_iota(jnp.int32, (tokens, tokens), 0)
    col = lax.broadcasted_iota(jnp.int32, (tokens, tokens), 1)
    allowed = (same > 0.5) & (col <= row)
    keys = key_value[:, :head]
    values = key_value[:, head:]
    mixed = []
    for g in range(groups):
        scores = dot(query[:, g * head : (g + 1) * head], keys, 1, 1) * scale
        scores = jnp.where(allowed, scores, -jnp.inf)
        power = jnp.exp(scores - jnp.max(scores, axis=1, keepdims=True))
        total = jnp.sum(power, axis=1, keepdims=True)
        mix = dot(power.astype(BF16), values, 1, 0)
        mixed.append((mix / total).astype(BF16))
    mixed = jnp.concatenate(mixed, axis=1)
    for t in range(parts):
        out[t] = dot(mixed, weight[:, t * share : (t + 1) * share], 1, 0).astype(BF16)


def queries_by_row(query, head):
    wide = query[...].astype(F32)
    groups = wide.shape[1] // head
    return jnp.concatenate(
        [wide[:, g * head : (g + 1) * head] for g in range(groups)], axis=0
    ).astype(BF16)


def before_kernel(length, query, own, cache, slots, frequency, top_o, total_o, mix_o, cos_o, sin_o):
    head = cache.shape[1] // 2
    decoders = query.shape[0]
    cache_len = cache.shape[0] // decoders
    scale = head**-0.5
    q = queries_by_row(query, head)
    rows = q.shape[0]
    listed = slots.shape[1]
    slot_col = jnp.broadcast_to(slots[...].astype(F32), (listed, listed)).T
    place = lax.broadcasted_iota(jnp.int32, (1, cache.shape[0]), 1).astype(F32)
    hit = jnp.max(jnp.where(slot_col[:, :1] == place, 1.0, 0.0), axis=0, keepdims=True)
    row = lax.broadcasted_iota(jnp.int32, (rows, cache.shape[0]), 0)
    col = lax.broadcasted_iota(jnp.int32, (rows, cache.shape[0]), 1)
    decoder = row % decoders
    offset = col - decoder * cache_len
    limit = jnp.full_like(row, length[0])
    for b in range(1, decoders):
        limit = jnp.where(decoder == b, length[b], limit)
    live = (offset >= 0) & (offset < limit) & (offset < cache_len) & (hit < 0.5)
    scores = dot(q, cache[:, :head], 1, 1) * scale
    scores = jnp.where(live, scores, -jnp.inf)
    pair = own[...].astype(F32)
    pair = jnp.concatenate([pair] * (rows // decoders), axis=0)
    self_score = jnp.sum(q.astype(F32) * pair[:, :head], axis=1, keepdims=True) * scale
    top = jnp.maximum(jnp.max(scores, axis=1, keepdims=True), self_score)
    power = jnp.exp(scores - top)
    own_power = jnp.exp(self_score - top)
    total = own_power + jnp.sum(power, axis=1, keepdims=True)
    mix = dot(power.astype(BF16), cache[:, head:], 1, 0)
    mix = mix + own_power.astype(BF16).astype(F32) * pair[:, head:]
    top_o[...] = jnp.broadcast_to(top, top_o.shape)
    total_o[...] = jnp.broadcast_to(total, total_o.shape)
    mix_o[...] = mix
    position = jnp.maximum(slot_col, 0.0)
    position = position - cache_len * jnp.floor(position * (1.0 / cache_len))
    angle = position * frequency[...]
    lane = lax.broadcasted_iota(jnp.int32, angle.shape, 1)
    cos_o[...] = jnp.cos(angle)
    sine = jnp.sin(angle)
    sin_o[...] = jnp.where(lane < head // 2, -sine, sine)


def after_kernel(length, got, query, slots, top_i, total_i, mix_i, cos_i, sin_i, weight, out):
    peers, cap, width = got.shape
    listed = slots.shape[1]
    head = mix_i.shape[1]
    decoders = query.shape[0]
    parts, _, share = out.shape
    cache_len = 512
    scale = head**-0.5
    flat = got[...].reshape(peers * cap, width)
    ordered = dot(flat[:, 2 * head :], flat[:, : 2 * head], 0, 0)
    key = ordered[:, :head]
    value = ordered[:, head:].astype(BF16)
    turned = (key * cos_i[...] + pltpu.roll(key, head // 2, 1) * sin_i[...]).astype(BF16)
    q = queries_by_row(query, head)
    rows = q.shape[0]
    scores = dot(q, turned, 1, 1) * scale
    row = lax.broadcasted_iota(jnp.int32, (rows, listed), 0)
    decoder = row % decoders
    limit = jnp.full_like(row, length[0])
    for b in range(1, decoders):
        limit = jnp.where(decoder == b, length[b], limit)
    offset = slots[...] - decoder * cache_len
    live = (slots[...] >= 0) & (offset >= 0) & (offset < limit) & (offset < cache_len)
    scores = jnp.where(live, scores, -jnp.inf)
    top = jnp.maximum(top_i[...], jnp.max(scores, axis=1, keepdims=True))
    power = jnp.exp(scores - top)
    keep = jnp.exp(top_i[...] - top)
    total = keep * total_i[...] + jnp.sum(power, axis=1, keepdims=True)
    mix = keep * mix_i[...] + dot(power.astype(BF16), value, 1, 0)
    mix = mix / total
    mixed = jnp.concatenate(
        [mix[i : i + decoders] for i in range(0, rows, decoders)], axis=1
    ).astype(BF16)
    for t in range(parts):
        out[t] = dot(mixed, weight[:, t * share : (t + 1) * share], 1, 0).astype(BF16)


def shards(
    prompt_query,
    prompt_key_value,
    prompt_segment_index,
    decoder_query,
    decoder_key_value,
    key_value_cache,
    live_cache_length,
    rebuild_hidden_state,
    owner_dest,
    miss_pos,
    key_value_weight,
    out_weight,
):
    pair = prompt_key_value.shape[-1]
    head = pair // 2
    peers = lax.axis_size("req")
    parts = lax.axis_size("tp")
    decoders = key_value_cache.shape[0]
    tokens = prompt_query.shape[0]
    listed = rebuild_hidden_state.shape[0]
    share = out_weight.shape[1] // parts
    shape = jax.ShapeDtypeStruct

    send = call(
        pack_kernel,
        shape((peers, CAP, pair + listed), BF16),
        rebuild_hidden_state,
        key_value_weight.reshape(-1, pair),
        owner_dest,
    )
    got = lax.all_to_all(send, "req", split_axis=0, concat_axis=0, tiled=True)

    prompt_part = call(
        prompt_kernel,
        shape((parts, tokens, share), BF16),
        prompt_query,
        prompt_key_value.reshape(tokens, pair),
        prompt_segment_index,
        out_weight,
    )
    half = head // 2
    frequency = (ROPE_BASE ** (-2.0 * (np.arange(head) % half) / head)).astype(np.float32)
    rows = decoder_query.shape[1] // head * decoders
    state = call(
        before_kernel,
        [shape((rows, head), F32)] * 3 + [shape((listed, head), F32)] * 2,
        decoder_query,
        decoder_key_value.reshape(decoders, pair),
        key_value_cache.reshape(-1, pair),
        miss_pos,
        jnp.asarray(frequency).reshape(1, head),
        scalars=(live_cache_length,),
    )
    prompt_got = lax.all_to_all(prompt_part, "tp", split_axis=0, concat_axis=0, tiled=True)
    dec_part = call(
        after_kernel,
        shape((parts, decoders, share), BF16),
        got,
        decoder_query,
        miss_pos,
        *state,
        out_weight,
        scalars=(live_cache_length,),
    )
    dec_got = lax.all_to_all(dec_part, "tp", split_axis=0, concat_axis=0, tiled=True)
    prompt_out = jnp.sum(prompt_got.astype(F32), axis=0).astype(BF16)
    dec_out = jnp.sum(dec_got.astype(F32), axis=0).astype(BF16)
    return prompt_out, dec_out


def solution(mesh):
    in_specs = (
        P("req", "tp"),
        P("req", "tp", None),
        P("req", None),
        P("req", "tp"),
        P("req", "tp", None),
        P("req", None, "tp", None),
        P("req"),
        P("req", None),
        P("req", None),
        P("req", None),
        P(None, "tp", None),
        P("tp", None),
    )
    out_specs = (P("req", "tp"), P("req", "tp"))
    return jax.shard_map(shards, mesh=mesh, in_specs=in_specs, out_specs=out_specs, check_vma=False)
```

```python
import jax
import jax.numpy as jnp
import numpy as np
from jax import lax
from jax.experimental import pallas as pl
from jax.experimental.pallas import tpu as pltpu
from jax.sharding import PartitionSpec as P

CAP = 2
ROPE_BASE = 600000.0
F32 = jnp.float32
BF16 = jnp.bfloat16


def dot(a, b, ca, cb):
    return lax.dot_general(a, b, (((ca,), (cb,)), ((), ())), preferred_element_type=F32)


def call(kernel, outs, *args, scalars=()):
    vmem = pl.BlockSpec(memory_space=pltpu.VMEM)
    smem = pl.BlockSpec(memory_space=pltpu.SMEM)
    return pl.pallas_call(
        kernel,
        out_shape=outs,
        in_specs=[smem] * len(scalars) + [vmem] * len(args),
        out_specs=jax.tree.map(lambda _: vmem, outs),
    )(*scalars, *args)


def pack_kernel(hidden, weight, dest, out):
    peers, cap, width = out.shape
    rows = hidden.shape[0]
    rebuilt = dot(hidden[...], weight[...], 1, 0).astype(BF16)
    number = lax.broadcasted_iota(jnp.int32, (1, rows), 1)
    code = dest[...] * cap + number % cap
    code = jnp.where(dest[...] >= 0, code, -1)
    place = lax.broadcasted_iota(jnp.int32, (peers * cap, rows), 0)
    chosen = jnp.where(place == code, 1.0, 0.0).astype(BF16)
    packed = dot(chosen, rebuilt, 1, 0).astype(BF16)
    both = jnp.concatenate([packed, chosen], axis=1)
    out[...] = both.reshape(peers, cap, width)


def prompt_kernel(place, query, key_value, segment, weight, *outs):
    tokens, _ = query.shape
    head = key_value.shape[1] // 2
    groups = query.shape[1] // head
    parts, share = len(outs), outs[0].shape[1]
    scale = head**-0.5
    same = jnp.where(
        lax.broadcasted_iota(jnp.int32, (8, tokens), 0) == segment[...], 1.0, 0.0
    ).astype(BF16)
    same = dot(same, same, 0, 0)
    row = lax.broadcasted_iota(jnp.int32, (tokens, tokens), 0)
    col = lax.broadcasted_iota(jnp.int32, (tokens, tokens), 1)
    allowed = (same > 0.5) & (col <= row)
    keys = key_value[:, :head]
    values = key_value[:, head:]
    mixed = []
    for g in range(groups):
        scores = dot(query[:, g * head : (g + 1) * head], keys, 1, 1) * scale
        scores = jnp.where(allowed, scores, -jnp.inf)
        power = jnp.exp(scores - jnp.max(scores, axis=1, keepdims=True))
        total = jnp.sum(power, axis=1, keepdims=True)
        mix = dot(power.astype(BF16), values, 1, 0)
        mixed.append((mix / total).astype(BF16))
    mixed = jnp.concatenate(mixed, axis=1)
    for k in range(parts):
        to = lax.rem(place[0] + k, parts)
        columns = pl.ds(pl.multiple_of(to * share, share), share)
        outs[k][...] = dot(mixed, weight[:, columns], 1, 0).astype(BF16)


def queries_by_row(query, head):
    wide = query[...].astype(F32)
    groups = wide.shape[1] // head
    return jnp.concatenate(
        [wide[:, g * head : (g + 1) * head] for g in range(groups)], axis=0
    ).astype(BF16)


def before_kernel(length, query, own, cache, slots, frequency, top_o, total_o, mix_o, cos_o, sin_o):
    head = cache.shape[1] // 2
    decoders = query.shape[0]
    cache_len = cache.shape[0] // decoders
    scale = head**-0.5
    q = queries_by_row(query, head)
    rows = q.shape[0]
    listed = slots.shape[1]
    slot_col = jnp.broadcast_to(slots[...].astype(F32), (listed, listed)).T
    place = lax.broadcasted_iota(jnp.int32, (1, cache.shape[0]), 1).astype(F32)
    hit = jnp.max(jnp.where(slot_col[:, :1] == place, 1.0, 0.0), axis=0, keepdims=True)
    row = lax.broadcasted_iota(jnp.int32, (rows, cache.shape[0]), 0)
    col = lax.broadcasted_iota(jnp.int32, (rows, cache.shape[0]), 1)
    decoder = row % decoders
    offset = col - decoder * cache_len
    limit = jnp.full_like(row, length[0])
    for b in range(1, decoders):
        limit = jnp.where(decoder == b, length[b], limit)
    live = (offset >= 0) & (offset < limit) & (offset < cache_len) & (hit < 0.5)
    scores = dot(q, cache[:, :head], 1, 1) * scale
    scores = jnp.where(live, scores, -jnp.inf)
    pair = own[...].astype(F32)
    pair = jnp.concatenate([pair] * (rows // decoders), axis=0)
    self_score = jnp.sum(q.astype(F32) * pair[:, :head], axis=1, keepdims=True) * scale
    top = jnp.maximum(jnp.max(scores, axis=1, keepdims=True), self_score)
    power = jnp.exp(scores - top)
    own_power = jnp.exp(self_score - top)
    total = own_power + jnp.sum(power, axis=1, keepdims=True)
    mix = dot(power.astype(BF16), cache[:, head:], 1, 0)
    mix = mix + own_power.astype(BF16).astype(F32) * pair[:, head:]
    top_o[...] = jnp.broadcast_to(top, top_o.shape)
    total_o[...] = jnp.broadcast_to(total, total_o.shape)
    mix_o[...] = mix
    position = jnp.maximum(slot_col, 0.0)
    position = position - cache_len * jnp.floor(position * (1.0 / cache_len))
    angle = position * frequency[...]
    lane = lax.broadcasted_iota(jnp.int32, angle.shape, 1)
    cos_o[...] = jnp.cos(angle)
    sine = jnp.sin(angle)
    sin_o[...] = jnp.where(lane < head // 2, -sine, sine)


def after_kernel(length, got, query, slots, top_i, total_i, mix_i, cos_i, sin_i, weight, out):
    peers, cap, width = got.shape
    listed = slots.shape[1]
    head = mix_i.shape[1]
    decoders = query.shape[0]
    parts, _, share = out.shape
    cache_len = 512
    scale = head**-0.5
    flat = got[...].reshape(peers * cap, width)
    ordered = dot(flat[:, 2 * head :], flat[:, : 2 * head], 0, 0)
    key = ordered[:, :head]
    value = ordered[:, head:].astype(BF16)
    turned = (key * cos_i[...] + pltpu.roll(key, head // 2, 1) * sin_i[...]).astype(BF16)
    q = queries_by_row(query, head)
    rows = q.shape[0]
    scores = dot(q, turned, 1, 1) * scale
    row = lax.broadcasted_iota(jnp.int32, (rows, listed), 0)
    decoder = row % decoders
    limit = jnp.full_like(row, length[0])
    for b in range(1, decoders):
        limit = jnp.where(decoder == b, length[b], limit)
    offset = slots[...] - decoder * cache_len
    live = (slots[...] >= 0) & (offset >= 0) & (offset < limit) & (offset < cache_len)
    scores = jnp.where(live, scores, -jnp.inf)
    top = jnp.maximum(top_i[...], jnp.max(scores, axis=1, keepdims=True))
    power = jnp.exp(scores - top)
    keep = jnp.exp(top_i[...] - top)
    total = keep * total_i[...] + jnp.sum(power, axis=1, keepdims=True)
    mix = keep * mix_i[...] + dot(power.astype(BF16), value, 1, 0)
    mix = mix / total
    mixed = jnp.concatenate(
        [mix[i : i + decoders] for i in range(0, rows, decoders)], axis=1
    ).astype(BF16)
    for t in range(parts):
        out[t] = dot(mixed, weight[:, t * share : (t + 1) * share], 1, 0).astype(BF16)


def shards(
    prompt_query,
    prompt_key_value,
    prompt_segment_index,
    decoder_query,
    decoder_key_value,
    key_value_cache,
    live_cache_length,
    rebuild_hidden_state,
    owner_dest,
    miss_pos,
    key_value_weight,
    out_weight,
):
    pair = prompt_key_value.shape[-1]
    head = pair // 2
    peers = lax.axis_size("req")
    parts = lax.axis_size("tp")
    decoders = key_value_cache.shape[0]
    tokens = prompt_query.shape[0]
    listed = rebuild_hidden_state.shape[0]
    share = out_weight.shape[1] // parts
    shape = jax.ShapeDtypeStruct

    send = call(
        pack_kernel,
        shape((peers, CAP, pair + listed), BF16),
        rebuild_hidden_state,
        key_value_weight.reshape(-1, pair),
        owner_dest,
    )
    got = lax.all_to_all(send, "req", split_axis=0, concat_axis=0, tiled=True)

    prompt_part = call(
        prompt_kernel,
        [shape((tokens, share), BF16)] * parts,
        prompt_query,
        prompt_key_value.reshape(tokens, pair),
        prompt_segment_index,
        out_weight,
        scalars=(lax.axis_index("tp").reshape(1),),
    )
    arrived = [
        lax.ppermute(prompt_part[k], "tp", [(i, (i + k) % parts) for i in range(parts)])
        for k in range(1, parts)
    ]
    half = head // 2
    frequency = (ROPE_BASE ** (-2.0 * (np.arange(head) % half) / head)).astype(np.float32)
    rows = decoder_query.shape[1] // head * decoders
    state = call(
        before_kernel,
        [shape((rows, head), F32)] * 3 + [shape((listed, head), F32)] * 2,
        decoder_query,
        decoder_key_value.reshape(decoders, pair),
        key_value_cache.reshape(-1, pair),
        miss_pos,
        jnp.asarray(frequency).reshape(1, head),
        scalars=(live_cache_length,),
    )
    dec_part = call(
        after_kernel,
        shape((parts, decoders, share), BF16),
        got,
        decoder_query,
        miss_pos,
        *state,
        out_weight,
        scalars=(live_cache_length,),
    )
    dec_got = lax.all_to_all(dec_part, "tp", split_axis=0, concat_axis=0, tiled=True)
    dec_out = jnp.sum(dec_got.astype(F32), axis=0).astype(BF16)
    prompt_out = prompt_part[0].astype(F32)
    for part in arrived:
        prompt_out = prompt_out + part.astype(F32)
    prompt_out = prompt_out.astype(BF16)
    return prompt_out, dec_out


def solution(mesh):
    in_specs = (
        P("req", "tp"),
        P("req", "tp", None),
        P("req", None),
        P("req", "tp"),
        P("req", "tp", None),
        P("req", None, "tp", None),
        P("req"),
        P("req", None),
        P("req", None),
        P("req", None),
        P(None, "tp", None),
        P("tp", None),
    )
    out_specs = (P("req", "tp"), P("req", "tp"))
    return jax.shard_map(shards, mesh=mesh, in_specs=in_specs, out_specs=out_specs, check_vma=False)
```

```python
import functools

import jax
import jax.numpy as jnp
import numpy as np
from jax import lax
from jax.experimental import pallas as pl
from jax.experimental.pallas import tpu as pltpu
from jax.sharding import PartitionSpec as P

CAP = 2
ROPE_BASE = 600000.0
VMEM_LIMIT = 16 * 2**20
F32 = jnp.float32
BF16 = jnp.bfloat16


def dot(a, b, ca, cb):
    return lax.dot_general(a, b, (((ca,), (cb,)), ((), ())), preferred_element_type=F32)


def near(x):
    return pltpu.with_memory_space_constraint(x, pltpu.VMEM)


def call(kernel, outs, *args):
    vmem = pl.BlockSpec(memory_space=pltpu.VMEM)
    return pl.pallas_call(
        kernel,
        out_shape=outs,
        in_specs=[vmem] * len(args),
        out_specs=jax.tree.map(lambda _: vmem, outs),
        compiler_params=pltpu.CompilerParams(vmem_limit_bytes=VMEM_LIMIT),
    )(*args)


def pack_kernel(count, *refs):
    hidden, weight, dest = refs[:3]
    later = refs[3 : 3 + count]
    out = refs[3 + count]
    kept = refs[4 + count : 4 + 2 * count]
    hidden_v, weight_v, dest_v, out_v, sem, later_sem = refs[4 + 2 * count :]
    peers, cap, _ = out.shape
    rows, depth = hidden.shape
    steps = 4
    step = depth // steps
    copies = [pltpu.make_async_copy(dest, dest_v, sem.at[2 * steps])]
    for k in range(steps):
        part = pl.ds(k * step, step)
        copies.append(pltpu.make_async_copy(hidden.at[:, part], hidden_v.at[:, part], sem.at[2 * k]))
        copies.append(pltpu.make_async_copy(weight.at[part], weight_v.at[part], sem.at[2 * k + 1]))
    copies += [
        pltpu.make_async_copy(x, y, later_sem.at[i])
        for i, (x, y) in enumerate(zip(later, kept, strict=True))
    ]
    own = 1 + 2 * steps
    for copy in copies[:own]:
        copy.start()
    copies[0].wait()
    number = lax.broadcasted_iota(jnp.int32, (1, rows), 1)
    code = dest_v[...] * cap + number % cap
    code = jnp.where(dest_v[...] >= 0, code, -1)
    place = lax.broadcasted_iota(jnp.int32, (peers * cap, rows), 0)
    chosen = jnp.where(place == code, 1.0, 0.0).astype(BF16)
    rebuilt = jnp.zeros((rows, weight.shape[1]), F32)
    for k in range(steps):
        copies[1 + 2 * k].wait()
        copies[2 + 2 * k].wait()
        if k == steps - 1:
            for copy in copies[own:]:
                copy.start()
        part = slice(k * step, (k + 1) * step)
        rebuilt = rebuilt + dot(hidden_v[:, part], weight_v[part], 1, 0)
    packed = dot(chosen, rebuilt.astype(BF16), 1, 0).astype(BF16)
    both = jnp.concatenate([packed, chosen], axis=1)
    out_v[...] = both.reshape(out.shape)
    send = pltpu.make_async_copy(out_v, out, sem.at[2 * steps + 1])
    send.start()
    for copy in copies[own:]:
        copy.wait()
    send.wait()


def pack(peers, hidden, weight, dest, *later):
    shape = (peers, CAP, weight.shape[1] + hidden.shape[0])
    vmem = pl.BlockSpec(memory_space=pltpu.VMEM)
    hbm = pl.BlockSpec(memory_space=pl.ANY)
    far = [
        pltpu.with_memory_space_constraint(x, pltpu.HBM)
        for x in (hidden, weight, dest, *later)
    ]
    send, *kept = pl.pallas_call(
        functools.partial(pack_kernel, len(later)),
        out_shape=[jax.ShapeDtypeStruct(shape, BF16)]
        + [pltpu.VMEM(x.shape, x.dtype) for x in later],
        in_specs=[hbm] * len(far),
        out_specs=[hbm] + [vmem] * len(later),
        scratch_shapes=[
            pltpu.VMEM(hidden.shape, BF16),
            pltpu.VMEM(weight.shape, BF16),
            pltpu.VMEM(dest.shape, dest.dtype),
            pltpu.VMEM(shape, BF16),
            pltpu.SemaphoreType.DMA((10,)),
            pltpu.SemaphoreType.DMA((len(later),)),
        ],
        compiler_params=pltpu.CompilerParams(vmem_limit_bytes=VMEM_LIMIT),
    )(*far)
    return send, kept


def prompt_kernel(query, key_value, segment, weight, *outs):
    tokens, _ = query.shape
    head = key_value.shape[1] // 2
    groups = query.shape[1] // head
    parts, share = len(outs), outs[0].shape[1]
    scale = head**-0.5
    same = jnp.where(
        lax.broadcasted_iota(jnp.int32, (8, tokens), 0) == segment[...], 1.0, 0.0
    ).astype(BF16)
    same = dot(same, same, 0, 0)
    row = lax.broadcasted_iota(jnp.int32, (tokens, tokens), 0)
    col = lax.broadcasted_iota(jnp.int32, (tokens, tokens), 1)
    allowed = (same > 0.5) & (col <= row)
    keys = key_value[:, :head]
    values = key_value[:, head:]
    mixed = []
    for g in range(groups):
        scores = dot(query[:, g * head : (g + 1) * head], keys, 1, 1) * scale
        scores = jnp.where(allowed, scores, -jnp.inf)
        power = jnp.exp(scores - jnp.max(scores, axis=1, keepdims=True))
        total = jnp.sum(power, axis=1, keepdims=True)
        mix = dot(power.astype(BF16), values, 1, 0)
        mixed.append((mix / total).astype(BF16))
    mixed = jnp.concatenate(mixed, axis=1)
    for k in range(parts):
        to = lax.rem(lax.axis_index("tp") + k, parts)
        columns = pl.ds(pl.multiple_of(to * share, share), share)
        outs[k][...] = dot(mixed, weight[:, columns], 1, 0).astype(BF16)


def queries_by_row(query, head):
    wide = query[...].astype(F32)
    groups = wide.shape[1] // head
    return jnp.concatenate(
        [wide[:, g * head : (g + 1) * head] for g in range(groups)], axis=0
    ).astype(BF16)


def before_kernel(length, query, own, cache, slots, frequency, top_o, total_o, mix_o, cos_o, sin_o):
    head = cache.shape[1] // 2
    decoders = query.shape[0]
    cache_len = cache.shape[0] // decoders
    scale = head**-0.5
    q = queries_by_row(query, head)
    rows = q.shape[0]
    listed = slots.shape[1]
    slot_col = jnp.broadcast_to(slots[...].astype(F32), (listed, listed)).T
    place = lax.broadcasted_iota(jnp.int32, (1, cache.shape[0]), 1).astype(F32)
    hit = jnp.max(jnp.where(slot_col[:, :1] == place, 1.0, 0.0), axis=0, keepdims=True)
    row = lax.broadcasted_iota(jnp.int32, (rows, cache.shape[0]), 0)
    col = lax.broadcasted_iota(jnp.int32, (rows, cache.shape[0]), 1)
    decoder = row % decoders
    offset = col - decoder * cache_len
    limit = length[:, :1]
    for b in range(1, decoders):
        limit = jnp.where(decoder == b, length[:, b : b + 1], limit)
    live = (offset >= 0) & (offset < limit) & (offset < cache_len) & (hit < 0.5)
    scores = dot(q, cache[:, :head], 1, 1) * scale
    scores = jnp.where(live, scores, -jnp.inf)
    pair = own[...].astype(F32)
    pair = jnp.concatenate([pair] * (rows // decoders), axis=0)
    self_score = jnp.sum(q.astype(F32) * pair[:, :head], axis=1, keepdims=True) * scale
    top = jnp.maximum(jnp.max(scores, axis=1, keepdims=True), self_score)
    power = jnp.exp(scores - top)
    own_power = jnp.exp(self_score - top)
    total = own_power + jnp.sum(power, axis=1, keepdims=True)
    mix = dot(power.astype(BF16), cache[:, head:], 1, 0)
    mix = mix + own_power.astype(BF16).astype(F32) * pair[:, head:]
    top_o[...] = jnp.broadcast_to(top, top_o.shape)
    total_o[...] = jnp.broadcast_to(total, total_o.shape)
    mix_o[...] = mix
    position = jnp.maximum(slot_col, 0.0)
    position = position - cache_len * jnp.floor(position * (1.0 / cache_len))
    angle = position * frequency[...]
    lane = lax.broadcasted_iota(jnp.int32, angle.shape, 1)
    cos_o[...] = jnp.cos(angle)
    sine = jnp.sin(angle)
    sin_o[...] = jnp.where(lane < head // 2, -sine, sine)


def after_kernel(cache_len, length, got, query, slots, top_i, total_i, mix_i, cos_i, sin_i, weight, out):
    peers, cap, width = got.shape
    listed = slots.shape[1]
    head = mix_i.shape[1]
    decoders = query.shape[0]
    parts, _, share = out.shape
    scale = head**-0.5
    flat = got[...].reshape(peers * cap, width)
    ordered = dot(flat[:, 2 * head :], flat[:, : 2 * head], 0, 0)
    key = ordered[:, :head]
    value = ordered[:, head:].astype(BF16)
    turned = (key * cos_i[...] + pltpu.roll(key, head // 2, 1) * sin_i[...]).astype(BF16)
    q = queries_by_row(query, head)
    rows = q.shape[0]
    scores = dot(q, turned, 1, 1) * scale
    row = lax.broadcasted_iota(jnp.int32, (rows, listed), 0)
    decoder = row % decoders
    limit = length[:, :1]
    for b in range(1, decoders):
        limit = jnp.where(decoder == b, length[:, b : b + 1], limit)
    offset = slots[...] - decoder * cache_len
    live = (slots[...] >= 0) & (offset >= 0) & (offset < limit) & (offset < cache_len)
    scores = jnp.where(live, scores, -jnp.inf)
    top = jnp.maximum(top_i[...], jnp.max(scores, axis=1, keepdims=True))
    power = jnp.exp(scores - top)
    keep = jnp.exp(top_i[...] - top)
    total = keep * total_i[...] + jnp.sum(power, axis=1, keepdims=True)
    mix = keep * mix_i[...] + dot(power.astype(BF16), value, 1, 0)
    mix = mix / total
    mixed = jnp.concatenate(
        [mix[i : i + decoders] for i in range(0, rows, decoders)], axis=1
    ).astype(BF16)
    for t in range(parts):
        out[t] = dot(mixed, weight[:, t * share : (t + 1) * share], 1, 0).astype(BF16)


def sum_kernel(*refs):
    *parts, out = refs
    total = parts[0][...].astype(F32)
    for part in parts[1:]:
        total = total + part[...].astype(F32)
    out[...] = total.astype(BF16)


def shards(
    prompt_query,
    prompt_key_value,
    prompt_segment_index,
    decoder_query,
    decoder_key_value,
    key_value_cache,
    live_cache_length,
    rebuild_hidden_state,
    owner_dest,
    miss_pos,
    key_value_weight,
    out_weight,
):
    pair = prompt_key_value.shape[-1]
    head = pair // 2
    peers = lax.axis_size("req")
    parts = lax.axis_size("tp")
    decoders = key_value_cache.shape[0]
    tokens = prompt_query.shape[0]
    listed = rebuild_hidden_state.shape[0]
    share = out_weight.shape[1] // parts
    shape = jax.ShapeDtypeStruct

    half = head // 2
    frequency = (ROPE_BASE ** (-2.0 * (np.arange(head) % half) / head)).astype(np.float32)
    send, kept = pack(
        peers,
        rebuild_hidden_state,
        key_value_weight.reshape(-1, pair),
        owner_dest,
        prompt_query,
        prompt_key_value.reshape(tokens, pair),
        prompt_segment_index,
        out_weight,
        key_value_cache.reshape(-1, pair),
        live_cache_length.reshape(1, decoders),
        decoder_query,
        decoder_key_value.reshape(decoders, pair),
        miss_pos,
        jnp.asarray(frequency).reshape(1, head),
    )
    got = lax.all_to_all(send, "req", split_axis=0, concat_axis=0, tiled=True)
    query_v, key_value_v, segment_v, weight_v, cache_v, length_v, dec_query_v, own_v, slots_v, frequency_v = map(near, kept)

    prompt_part = call(
        prompt_kernel,
        [shape((tokens, share), BF16)] * parts,
        query_v,
        key_value_v,
        segment_v,
        weight_v,
    )
    arrived = [
        lax.ppermute(prompt_part[k], "tp", [(i, (i + k) % parts) for i in range(parts)])
        for k in range(1, parts)
    ]
    rows = decoder_query.shape[1] // head * decoders
    state = call(
        before_kernel,
        [pltpu.VMEM((rows, head), F32)] * 3 + [pltpu.VMEM((listed, head), F32)] * 2,
        length_v,
        dec_query_v,
        own_v,
        cache_v,
        slots_v,
        frequency_v,
    )
    dec_part = call(
        functools.partial(after_kernel, key_value_cache.shape[1]),
        shape((parts, decoders, share), BF16),
        length_v,
        near(got),
        dec_query_v,
        slots_v,
        *map(near, state),
        weight_v,
    )
    dec_got = lax.all_to_all(dec_part, "tp", split_axis=0, concat_axis=0, tiled=True)
    dec_out = jnp.sum(dec_got.astype(F32), axis=0).astype(BF16)
    prompt_out = call(
        sum_kernel, shape((tokens, share), BF16), prompt_part[0], *map(near, arrived)
    )
    return prompt_out, dec_out


def solution(mesh):
    in_specs = (
        P("req", "tp"),
        P("req", "tp", None),
        P("req", None),
        P("req", "tp"),
        P("req", "tp", None),
        P("req", None, "tp", None),
        P("req"),
        P("req", None),
        P("req", None),
        P("req", None),
        P(None, "tp", None),
        P("tp", None),
    )
    out_specs = (P("req", "tp"), P("req", "tp"))
    return jax.shard_map(shards, mesh=mesh, in_specs=in_specs, out_specs=out_specs, check_vma=False)
```

```python
import functools

import jax
import jax.numpy as jnp
import numpy as np
from jax import lax
from jax.experimental import pallas as pl
from jax.experimental.pallas import tpu as pltpu
from jax.sharding import PartitionSpec as P

CAP = 2
ROPE_BASE = 600000.0
VMEM_LIMIT = 16 * 2**20
F32 = jnp.float32
BF16 = jnp.bfloat16


def dot(a, b, ca, cb):
    return lax.dot_general(a, b, (((ca,), (cb,)), ((), ())), preferred_element_type=F32)


def like(x):
    return pltpu.VMEM(x.shape, x.dtype)


def near(x):
    return pltpu.with_memory_space_constraint(x, pltpu.VMEM)


def call(kernel, outs, *args, far=(), scratch=(), far_out=0):
    vmem = pl.BlockSpec(memory_space=pltpu.VMEM)
    hbm = pl.BlockSpec(memory_space=pl.ANY)
    return pl.pallas_call(
        kernel,
        out_shape=list(outs),
        in_specs=[vmem] * len(args) + [hbm] * len(far),
        out_specs=[hbm] * far_out + [vmem] * (len(outs) - far_out),
        scratch_shapes=scratch,
        compiler_params=pltpu.CompilerParams(vmem_limit_bytes=VMEM_LIMIT),
    )(*map(near, args), *[pltpu.with_memory_space_constraint(x, pltpu.HBM) for x in far])


def start_all(far, near_refs, sem):
    copies = [
        pltpu.make_async_copy(x, y, sem.at[i]) for i, (x, y) in enumerate(zip(far, near_refs, strict=True))
    ]
    for copy in copies:
        copy.start()
    return copies


def columns_for(k, share, parts):
    to = lax.bitwise_xor(lax.axis_index("tp"), k)
    return pl.ds(pl.multiple_of(to * share, share), share)


def pack_kernel(hidden, weight, dest, out, hidden_v, weight_v, dest_v, out_v, sem):
    peers, cap, width = out.shape
    rows, depth = hidden.shape
    steps, halves = 4, 2
    part = [pl.ds(k * depth // steps, depth // steps) for k in range(steps)]
    copies = start_all(
        [dest, *[x for p in part for x in (hidden.at[:, p], weight.at[p])]],
        [dest_v, *[x for p in part for x in (hidden_v.at[:, p], weight_v.at[p])]],
        sem,
    )
    copies[0].wait()
    number = lax.broadcasted_iota(jnp.int32, (1, rows), 1)
    code = dest_v[...] * cap + number % cap
    code = jnp.where(dest_v[...] >= 0, code, -1)
    place = lax.broadcasted_iota(jnp.int32, (peers * cap, rows), 0)
    chosen = jnp.where(place == code, 1.0, 0.0).astype(BF16)
    rebuilt = jnp.zeros((rows, weight.shape[1]), F32)
    for k, p in enumerate(part):
        copies[1 + 2 * k].wait()
        copies[2 + 2 * k].wait()
        rebuilt = rebuilt + dot(hidden_v[:, p], weight_v[p], 1, 0)
    rebuilt = rebuilt.astype(BF16)
    sends = []
    for h in range(halves):
        size = peers // halves
        mine = chosen[h * size * cap : (h + 1) * size * cap]
        packed = dot(mine, rebuilt, 1, 0).astype(BF16)
        own = pl.ds(h * size, size)
        out_v[own] = jnp.concatenate([packed, mine], axis=1).reshape(size, cap, width)
        sends.append(pltpu.make_async_copy(out_v.at[own], out.at[own], sem.at[1 + 2 * steps + h]))
        sends[-1].start()
    for send in sends:
        send.wait()


def middle_kernel(parts, query, key_value, segment, weight, *refs):
    blocks = 8
    far, outs, weight_o = refs[:6], refs[6 : 13 + parts], refs[13 + parts]
    held, sem = refs[14 + parts : 23 + parts], refs[23 + parts]
    step = weight.shape[0] // blocks
    block = [pl.ds(i * step, step) for i in range(blocks)]
    copies = start_all(
        [query, key_value, segment, *[weight.at[x] for x in block], *far],
        [*held[:3], *[weight_o.at[x] for x in block], *held[3:]],
        sem,
    )
    for copy in copies[:3]:
        copy.wait()
    mixed = prompt_rows(*held[:3])
    for copy in copies[3:]:
        copy.wait()
    share = outs[0].shape[1]
    for k in range(parts):
        outs[k][...] = dot(mixed, weight_o[:, columns_for(k, share, parts)], 1, 0).astype(BF16)
    cache_rows(*held[3:], *outs[parts:])


def prompt_rows(query, key_value, segment):
    tokens, _ = query.shape
    head = key_value.shape[1] // 2
    groups = query.shape[1] // head
    scale = head**-0.5
    same = jnp.where(
        lax.broadcasted_iota(jnp.int32, (8, tokens), 0) == segment[...], 1.0, 0.0
    ).astype(BF16)
    same = dot(same, same, 0, 0)
    row = lax.broadcasted_iota(jnp.int32, (tokens, tokens), 0)
    col = lax.broadcasted_iota(jnp.int32, (tokens, tokens), 1)
    allowed = (same > 0.5) & (col <= row)
    keys = key_value[:, :head]
    values = key_value[:, head:]
    mixed = []
    for g in range(groups):
        scores = dot(query[:, g * head : (g + 1) * head], keys, 1, 1) * scale
        scores = jnp.where(allowed, scores, -jnp.inf)
        power = jnp.exp(scores - jnp.max(scores, axis=1, keepdims=True))
        total = jnp.sum(power, axis=1, keepdims=True)
        mix = dot(power.astype(BF16), values, 1, 0)
        mixed.append((mix / total).astype(BF16))
    return jnp.concatenate(mixed, axis=1)


def queries_by_row(query, head):
    wide = query[...].astype(F32)
    groups = wide.shape[1] // head
    return jnp.concatenate(
        [wide[:, g * head : (g + 1) * head] for g in range(groups)], axis=0
    ).astype(BF16)


def cache_rows(cache, length, query, own, slots, frequency, query_o, live_o, top_o, total_o, mix_o, cos_o, sin_o):
    head = cache.shape[1] // 2
    decoders = query.shape[0]
    cache_len = cache.shape[0] // decoders
    scale = head**-0.5
    q = queries_by_row(query, head)
    rows = q.shape[0]
    listed = slots.shape[1]
    slot_col = jnp.broadcast_to(slots[...].astype(F32), (listed, listed)).T
    place = lax.broadcasted_iota(jnp.int32, (1, cache.shape[0]), 1).astype(F32)
    hit = jnp.max(jnp.where(slot_col[:, :1] == place, 1.0, 0.0), axis=0, keepdims=True)

    def is_live(slot):
        decoder = lax.broadcasted_iota(jnp.int32, (rows, slot.shape[1]), 0) % decoders
        offset = slot - decoder * cache_len
        limit = length[:, :1]
        for b in range(1, decoders):
            limit = jnp.where(decoder == b, length[:, b : b + 1], limit)
        return (offset >= 0) & (offset < limit) & (offset < cache_len)

    query_o[...] = q
    listed_live = is_live(slots[...]) & (slots[...] >= 0)
    live_o[...] = jnp.where(listed_live, 0.0, -jnp.inf)
    col = lax.broadcasted_iota(jnp.int32, (1, cache.shape[0]), 1)
    live = is_live(col) & (hit < 0.5)
    scores = dot(q, cache[:, :head], 1, 1) * scale
    scores = jnp.where(live, scores, -jnp.inf)
    pair = own[...].astype(F32)
    pair = jnp.concatenate([pair] * (rows // decoders), axis=0)
    self_score = jnp.sum(q.astype(F32) * pair[:, :head], axis=1, keepdims=True) * scale
    top = jnp.maximum(jnp.max(scores, axis=1, keepdims=True), self_score)
    power = jnp.exp(scores - top)
    own_power = jnp.exp(self_score - top)
    total = own_power + jnp.sum(power, axis=1, keepdims=True)
    mix = dot(power.astype(BF16), cache[:, head:], 1, 0)
    mix = mix + own_power.astype(BF16).astype(F32) * pair[:, head:]
    top_o[...] = jnp.broadcast_to(top, top_o.shape)
    total_o[...] = jnp.broadcast_to(total, total_o.shape)
    mix_o[...] = mix
    position = jnp.maximum(slot_col, 0.0)
    position = position - cache_len * jnp.floor(position * (1.0 / cache_len))
    angle = position * frequency[...]
    lane = lax.broadcasted_iota(jnp.int32, angle.shape, 1)
    cos_o[...] = jnp.cos(angle)
    sine = jnp.sin(angle)
    sin_o[...] = jnp.where(lane < head // 2, -sine, sine)


def after_kernel(decoders, got, query, live, top_i, total_i, mix_i, cos_i, sin_i, weight, out):
    peers, cap, width = got.shape
    rows, head = mix_i.shape
    parts, _, share = out.shape
    scale = head**-0.5
    flat = got[...].reshape(peers * cap, width)
    ordered = dot(flat[:, 2 * head :], flat[:, : 2 * head], 0, 0)
    key = ordered[:, :head]
    value = ordered[:, head:].astype(BF16)
    turned = (key * cos_i[...] + pltpu.roll(key, head // 2, 1) * sin_i[...]).astype(BF16)
    scores = dot(query[...], turned, 1, 1) * scale + live[...]
    top = jnp.maximum(top_i[...], jnp.max(scores, axis=1, keepdims=True))
    power = jnp.exp(scores - top)
    keep = jnp.exp(top_i[...] - top)
    total = keep * total_i[...] + jnp.sum(power, axis=1, keepdims=True)
    mix = keep * mix_i[...] + dot(power.astype(BF16), value, 1, 0)
    mix = mix / total
    mixed = jnp.concatenate(
        [mix[i : i + decoders] for i in range(0, rows, decoders)], axis=1
    ).astype(BF16)
    for t in range(parts):
        out[t] = dot(mixed, weight[:, t * share : (t + 1) * share], 1, 0).astype(BF16)


def sum_kernel(*refs):
    *parts, out = refs
    total = parts[0][...].astype(F32)
    for part in parts[1:]:
        total = total + part[...].astype(F32)
    out[...] = total.astype(BF16)


def shards(
    prompt_query,
    prompt_key_value,
    prompt_segment_index,
    decoder_query,
    decoder_key_value,
    key_value_cache,
    live_cache_length,
    rebuild_hidden_state,
    owner_dest,
    miss_pos,
    key_value_weight,
    out_weight,
):
    pair = prompt_key_value.shape[-1]
    head = pair // 2
    peers = lax.axis_size("req")
    parts = lax.axis_size("tp")
    decoders = key_value_cache.shape[0]
    tokens = prompt_query.shape[0]
    listed = rebuild_hidden_state.shape[0]
    share = out_weight.shape[1] // parts
    shape = jax.ShapeDtypeStruct

    half = head // 2
    frequency = (ROPE_BASE ** (-2.0 * (np.arange(head) % half) / head)).astype(np.float32)
    rows = decoder_query.shape[1] // head * decoders
    payload = (peers, CAP, pair + listed)
    far = (rebuild_hidden_state, key_value_weight.reshape(-1, pair), owner_dest)
    (send,) = call(
        pack_kernel,
        [shape(payload, BF16)],
        far=far,
        scratch=[*map(like, far), pltpu.VMEM(payload, BF16), pltpu.SemaphoreType.DMA((11,))],
        far_out=1,
    )
    got = lax.all_to_all(send, "req", split_axis=0, concat_axis=0, tiled=True)
    far = (
        prompt_query,
        prompt_key_value.reshape(tokens, pair),
        prompt_segment_index,
        out_weight,
        key_value_cache.reshape(-1, pair),
        live_cache_length.reshape(1, decoders),
        decoder_query,
        decoder_key_value.reshape(decoders, pair),
        miss_pos,
        jnp.asarray(frequency).reshape(1, head),
    )
    middle = call(
        functools.partial(middle_kernel, parts),
        [pltpu.VMEM((tokens, share), BF16)] * parts
        + [pltpu.VMEM((rows, head), BF16), pltpu.VMEM((rows, listed), F32)]
        + [pltpu.VMEM((rows, head), F32)] * 3
        + [pltpu.VMEM((listed, head), F32)] * 2
        + [like(out_weight)],
        far=far,
        scratch=[like(x) for x in far if x is not out_weight] + [pltpu.SemaphoreType.DMA((17,))],
    )
    prompt_part, state = middle[:parts], middle[parts:]
    arrived = [
        lax.ppermute(prompt_part[k], "tp", [(i, i ^ k) for i in range(parts)])
        for k in (2, 1, 3)
    ]
    (dec_part,) = call(
        functools.partial(after_kernel, decoders),
        [pltpu.VMEM((parts, decoders, share), BF16)],
        got,
        *state,
    )
    dec_got = lax.all_to_all(dec_part, "tp", split_axis=0, concat_axis=0, tiled=True)
    dec_out = jnp.sum(dec_got.astype(F32), axis=0).astype(BF16)
    (prompt_out,) = call(sum_kernel, [shape((tokens, share), BF16)], prompt_part[0], *arrived)
    return prompt_out, dec_out


def solution(mesh):
    in_specs = (
        P("req", "tp"),
        P("req", "tp", None),
        P("req", None),
        P("req", "tp"),
        P("req", "tp", None),
        P("req", None, "tp", None),
        P("req"),
        P("req", None),
        P("req", None),
        P("req", None),
        P(None, "tp", None),
        P("tp", None),
    )
    out_specs = (P("req", "tp"), P("req", "tp"))
    return jax.shard_map(shards, mesh=mesh, in_specs=in_specs, out_specs=out_specs, check_vma=False)
```

```python
import functools

import jax
import jax.numpy as jnp
import numpy as np
from jax import lax
from jax.experimental import pallas as pl
from jax.experimental.pallas import tpu as pltpu
from jax.sharding import PartitionSpec as P

CAP = 2
ROPE_BASE = 600000.0
VMEM_LIMIT = 16 * 2**20
STRIDE = 37
F32 = jnp.float32
BF16 = jnp.bfloat16


def dot(a, b, ca, cb):
    return lax.dot_general(a, b, (((ca,), (cb,)), ((), ())), preferred_element_type=F32)


def like(x):
    return pltpu.VMEM(x.shape, x.dtype)


def near(x):
    return pltpu.with_memory_space_constraint(x, pltpu.VMEM)


def call(kernel, outs, *args, far=(), scratch=(), far_out=0):
    vmem = pl.BlockSpec(memory_space=pltpu.VMEM)
    hbm = pl.BlockSpec(memory_space=pl.ANY)
    return pl.pallas_call(
        kernel,
        out_shape=list(outs),
        in_specs=[vmem] * len(args) + [hbm] * len(far),
        out_specs=[hbm] * far_out + [vmem] * (len(outs) - far_out),
        scratch_shapes=scratch,
        compiler_params=pltpu.CompilerParams(vmem_limit_bytes=VMEM_LIMIT),
    )(*map(near, args), *[pltpu.with_memory_space_constraint(x, pltpu.HBM) for x in far])


def start_all(far, near_refs, sem):
    copies = [
        pltpu.make_async_copy(x, y, sem.at[i]) for i, (x, y) in enumerate(zip(far, near_refs, strict=True))
    ]
    for copy in copies:
        copy.start()
    return copies


def columns_for(k, share, parts):
    to = lax.bitwise_xor(lax.axis_index("tp"), k)
    return pl.ds(pl.multiple_of(to * share, share), share)


def pack_kernel(
    hidden, weight, dest, query, key_value, segment, out, query_o, key_value_o, segment_o,
    hidden_v, weight_v, dest_v, out_v, sem, later_sem,
):
    peers, cap, width = out.shape
    rows, depth = hidden.shape
    steps, halves = 4, 2
    part = [pl.ds(k * depth // steps, depth // steps) for k in range(steps)]
    copies = start_all(
        [dest, *[x for p in part for x in (hidden.at[:, p], weight.at[p])]],
        [dest_v, *[x for p in part for x in (hidden_v.at[:, p], weight_v.at[p])]],
        sem,
    )
    copies[0].wait()
    number = lax.broadcasted_iota(jnp.int32, (1, rows), 1)
    member = ((peers - 1 - dest_v[...]) * pow(STRIDE, -1, peers)) % peers
    code = member * cap + number % cap
    code = jnp.where(dest_v[...] >= 0, code, -1)
    place = lax.broadcasted_iota(jnp.int32, (peers * cap, rows), 0)
    chosen = jnp.where(place == code, 1.0, 0.0).astype(BF16)
    rebuilt = jnp.zeros((rows, weight.shape[1]), F32)
    for k, p in enumerate(part):
        copies[1 + 2 * k].wait()
        copies[2 + 2 * k].wait()
        rebuilt = rebuilt + dot(hidden_v[:, p], weight_v[p], 1, 0)
    rebuilt = rebuilt.astype(BF16)
    later = start_all((query, key_value, segment), (query_o, key_value_o, segment_o), later_sem)
    sends = []
    for h in range(halves):
        size = peers // halves
        mine = chosen[h * size * cap : (h + 1) * size * cap]
        packed = dot(mine, rebuilt, 1, 0).astype(BF16)
        own = pl.ds(h * size, size)
        out_v[own] = jnp.concatenate([packed, mine], axis=1).reshape(size, cap, width)
        sends.append(pltpu.make_async_copy(out_v.at[own], out.at[own], sem.at[1 + 2 * steps + h]))
        sends[-1].start()
    for copy in sends + later:
        copy.wait()


def middle_kernel(parts, query, key_value, segment, weight, *refs):
    far, outs, held, sem = refs[:6], refs[6 : 13 + parts], refs[13 + parts : 19 + parts], refs[19 + parts]
    copies = start_all(far, held, sem)
    mixed = prompt_rows(query, key_value, segment)
    share = outs[0].shape[1]
    for k in range(parts):
        outs[k][...] = dot(mixed, weight[:, columns_for(k, share, parts)], 1, 0).astype(BF16)
    for copy in copies:
        copy.wait()
    cache_rows(*held, *outs[parts:])


def prompt_rows(query, key_value, segment):
    tokens, _ = query.shape
    head = key_value.shape[1] // 2
    groups = query.shape[1] // head
    scale = head**-0.5
    same = jnp.where(
        lax.broadcasted_iota(jnp.int32, (8, tokens), 0) == segment[...], 1.0, 0.0
    ).astype(BF16)
    same = dot(same, same, 0, 0)
    row = lax.broadcasted_iota(jnp.int32, (tokens, tokens), 0)
    col = lax.broadcasted_iota(jnp.int32, (tokens, tokens), 1)
    allowed = (same > 0.5) & (col <= row)
    keys = key_value[:, :head]
    values = key_value[:, head:]
    mixed = []
    for g in range(groups):
        scores = dot(query[:, g * head : (g + 1) * head], keys, 1, 1) * scale
        scores = jnp.where(allowed, scores, -jnp.inf)
        power = jnp.exp(scores - jnp.max(scores, axis=1, keepdims=True))
        total = jnp.sum(power, axis=1, keepdims=True)
        mix = dot(power.astype(BF16), values, 1, 0)
        mixed.append((mix / total).astype(BF16))
    return jnp.concatenate(mixed, axis=1)


def queries_by_row(query, head):
    wide = query[...].astype(F32)
    groups = wide.shape[1] // head
    return jnp.concatenate(
        [wide[:, g * head : (g + 1) * head] for g in range(groups)], axis=0
    ).astype(BF16)


def cache_rows(cache, length, query, own, slots, frequency, query_o, live_o, top_o, total_o, mix_o, cos_o, sin_o):
    head = cache.shape[1] // 2
    decoders = query.shape[0]
    cache_len = cache.shape[0] // decoders
    scale = head**-0.5
    q = queries_by_row(query, head)
    rows = q.shape[0]
    listed = slots.shape[1]
    slot_col = jnp.broadcast_to(slots[...].astype(F32), (listed, listed)).T
    place = lax.broadcasted_iota(jnp.int32, (1, cache.shape[0]), 1).astype(F32)
    hit = jnp.max(jnp.where(slot_col[:, :1] == place, 1.0, 0.0), axis=0, keepdims=True)

    def is_live(slot):
        decoder = lax.broadcasted_iota(jnp.int32, (rows, slot.shape[1]), 0) % decoders
        offset = slot - decoder * cache_len
        limit = length[:, :1]
        for b in range(1, decoders):
            limit = jnp.where(decoder == b, length[:, b : b + 1], limit)
        return (offset >= 0) & (offset < limit) & (offset < cache_len)

    query_o[...] = q
    listed_live = is_live(slots[...]) & (slots[...] >= 0)
    live_o[...] = jnp.where(listed_live, 0.0, -jnp.inf)
    col = lax.broadcasted_iota(jnp.int32, (1, cache.shape[0]), 1)
    live = is_live(col) & (hit < 0.5)
    scores = dot(q, cache[:, :head], 1, 1) * scale
    scores = jnp.where(live, scores, -jnp.inf)
    pair = own[...].astype(F32)
    pair = jnp.concatenate([pair] * (rows // decoders), axis=0)
    self_score = jnp.sum(q.astype(F32) * pair[:, :head], axis=1, keepdims=True) * scale
    top = jnp.maximum(jnp.max(scores, axis=1, keepdims=True), self_score)
    power = jnp.exp(scores - top)
    own_power = jnp.exp(self_score - top)
    total = own_power + jnp.sum(power, axis=1, keepdims=True)
    mix = dot(power.astype(BF16), cache[:, head:], 1, 0)
    mix = mix + own_power.astype(BF16).astype(F32) * pair[:, head:]
    top_o[...] = jnp.broadcast_to(top, top_o.shape)
    total_o[...] = jnp.broadcast_to(total, total_o.shape)
    mix_o[...] = mix
    position = jnp.maximum(slot_col, 0.0)
    position = position - cache_len * jnp.floor(position * (1.0 / cache_len))
    angle = position * frequency[...]
    lane = lax.broadcasted_iota(jnp.int32, angle.shape, 1)
    cos_o[...] = jnp.cos(angle)
    sine = jnp.sin(angle)
    sin_o[...] = jnp.where(lane < head // 2, -sine, sine)


def after_kernel(decoders, got, query, live, top_i, total_i, mix_i, cos_i, sin_i, weight, out):
    peers, cap, width = got.shape
    rows, head = mix_i.shape
    parts, _, share = out.shape
    scale = head**-0.5
    flat = got[...].reshape(peers * cap, width)
    ordered = dot(flat[:, 2 * head :], flat[:, : 2 * head], 0, 0)
    key = ordered[:, :head]
    value = ordered[:, head:].astype(BF16)
    turned = (key * cos_i[...] + pltpu.roll(key, head // 2, 1) * sin_i[...]).astype(BF16)
    scores = dot(query[...], turned, 1, 1) * scale + live[...]
    top = jnp.maximum(top_i[...], jnp.max(scores, axis=1, keepdims=True))
    power = jnp.exp(scores - top)
    keep = jnp.exp(top_i[...] - top)
    total = keep * total_i[...] + jnp.sum(power, axis=1, keepdims=True)
    mix = keep * mix_i[...] + dot(power.astype(BF16), value, 1, 0)
    mix = mix / total
    mixed = jnp.concatenate(
        [mix[i : i + decoders] for i in range(0, rows, decoders)], axis=1
    ).astype(BF16)
    for t in range(parts):
        out[t] = dot(mixed, weight[:, t * share : (t + 1) * share], 1, 0).astype(BF16)


def sum_kernel(own, *refs):
    *arrived, dec, prompt_out, dec_out = refs
    total = own[...].astype(F32)
    for part in arrived:
        total = total + part[...].astype(F32)
    prompt_out[...] = total.astype(BF16)
    dec_out[...] = dec[...]


def shards(
    prompt_query,
    prompt_key_value,
    prompt_segment_index,
    decoder_query,
    decoder_key_value,
    key_value_cache,
    live_cache_length,
    rebuild_hidden_state,
    owner_dest,
    miss_pos,
    key_value_weight,
    out_weight,
):
    pair = prompt_key_value.shape[-1]
    head = pair // 2
    peers = lax.axis_size("req")
    parts = lax.axis_size("tp")
    decoders = key_value_cache.shape[0]
    tokens = prompt_query.shape[0]
    listed = rebuild_hidden_state.shape[0]
    share = out_weight.shape[1] // parts
    shape = jax.ShapeDtypeStruct

    half = head // 2
    frequency = (ROPE_BASE ** (-2.0 * (np.arange(head) % half) / head)).astype(np.float32)
    rows = decoder_query.shape[1] // head * decoders
    payload = (peers, CAP, pair + listed)
    far = (rebuild_hidden_state, key_value_weight.reshape(-1, pair), owner_dest)
    later = (prompt_query, prompt_key_value.reshape(tokens, pair), prompt_segment_index)
    send, *kept = call(
        pack_kernel,
        [shape(payload, BF16), *map(like, later)],
        far=far + later,
        scratch=[*map(like, far), pltpu.VMEM(payload, BF16)]
        + [pltpu.SemaphoreType.DMA((11,)), pltpu.SemaphoreType.DMA((3,))],
        far_out=1,
    )
    members = [peers - 1 - (STRIDE * i) % peers for i in range(peers)]
    got = lax.all_to_all(
        send, "req", split_axis=0, concat_axis=0, tiled=True, axis_index_groups=[members]
    )
    far = (
        key_value_cache.reshape(-1, pair),
        live_cache_length.reshape(1, decoders),
        decoder_query,
        decoder_key_value.reshape(decoders, pair),
        miss_pos,
        jnp.asarray(frequency).reshape(1, head),
    )
    middle = call(
        functools.partial(middle_kernel, parts),
        [pltpu.VMEM((tokens, share), BF16)] * parts
        + [pltpu.VMEM((rows, head), BF16), pltpu.VMEM((rows, listed), F32)]
        + [pltpu.VMEM((rows, head), F32)] * 3
        + [pltpu.VMEM((listed, head), F32)] * 2,
        *kept,
        out_weight,
        far=far,
        scratch=[*map(like, far), pltpu.SemaphoreType.DMA((len(far),))],
    )
    prompt_part, state = middle[:parts], middle[parts:]
    arrived = [
        lax.ppermute(prompt_part[k], "tp", [(i, i ^ k) for i in range(parts)])
        for k in (2, 1, 3)
    ]
    (dec_part,) = call(
        functools.partial(after_kernel, decoders),
        [pltpu.VMEM((parts, decoders, share), BF16)],
        got,
        *state,
        out_weight,
    )
    dec_got = lax.all_to_all(dec_part, "tp", split_axis=0, concat_axis=0, tiled=True)
    dec_out = jnp.sum(dec_got.astype(F32), axis=0).astype(BF16)
    own_part, dec_out = lax.optimization_barrier((prompt_part[0], dec_out))
    prompt_out, dec_out = call(
        sum_kernel,
        [shape((tokens, share), BF16), shape((decoders, share), BF16)],
        own_part,
        *arrived,
        dec_out,
    )
    return prompt_out, dec_out


def solution(mesh):
    in_specs = (
        P("req", "tp"),
        P("req", "tp", None),
        P("req", None),
        P("req", "tp"),
        P("req", "tp", None),
        P("req", None, "tp", None),
        P("req"),
        P("req", None),
        P("req", None),
        P("req", None),
        P(None, "tp", None),
        P("tp", None),
    )
    out_specs = (P("req", "tp"), P("req", "tp"))
    return jax.shard_map(shards, mesh=mesh, in_specs=in_specs, out_specs=out_specs, check_vma=False)
```
